32 devices in a mesh: groups: 2 (over y), wide: 4 (over z), narrow: 4 (over x, core).
Axes of the slice: x: 2, y: 2, z: 4, core: 2. Of those that a mesh axis runs over, the one named last changes fastest.
Arguments:
- inputs: bfloat16 [40, 2, 8192], P('groups', None, 'narrow'), parts along dimension 0, may hold values from -6 to 6
- xz_weight: bfloat16 [8192, 2, 16384], P('narrow', None, 'wide'), may hold values from -0.0625 to 0.0625
- bc_weight: bfloat16 [8192, 4096], P('narrow', 'wide'), may hold values from -0.0625 to 0.0625
- dt_weight: bfloat16 [8192, 256], P('narrow', 'wide'), may hold values from -0.0625 to 0.0625
- conv_x_weight: bfloat16 [4, 256, 64], P(None, 'wide', 'narrow'), may hold values from -3 to 3
- conv_x_bias: bfloat16 [256, 64], P('wide', 'narrow'), may hold values from -3 to 3
- conv_bc_weight: bfloat16 [4, 4096], P(None, 'wide'), may hold values from -3 to 3
- conv_bc_bias: bfloat16 [4096], P('wide'), may hold values from -3 to 3
- conv_x_state: bfloat16 [40, 3, 256, 64], P('groups', None, 'wide', 'narrow'), parts along dimension 0, may hold values from -6 to 6
- conv_bc_state: bfloat16 [40, 3, 4096], P('groups', None, 'wide'), parts along dimension 0, may hold values from -6 to 6
- dt_bias: float32 [256], P('wide'), may hold values from -4 to 0
- a_log: float32 [256], P('wide'), may hold values from 0 to 2.5
- d_skip: float32 [256], P('wide'), may hold values from 0.5 to 2
- norm_weight: bfloat16 [256, 64], P('wide', 'narrow'), may hold values from 0.099609375 to 1.8984375
- out_weight: bfloat16 [256, 64, 8192], P(None, 'narrow', 'wide'), may hold values from -0.046875 to 0.046875
- ssm_state: float32 [40, 256, 64, 256], P('groups', 'wide', 'narrow'), parts along dimension 0, may hold values from -4 to 4
Outputs:
- layer_out: bfloat16 [40, 2, 8192], P('groups', None, ('wide', 'narrow')), parts along dimension 0
- new_ssm_state: float32 [40, 256, 64, 256], P('groups', 'wide', 'narrow'), parts along dimension 0
- new_conv_x: bfloat16 [40, 3, 256, 64], P('groups', None, 'wide', 'narrow'), parts along dimension 0
- new_conv_bc: bfloat16 [40, 3, 4096], P('groups', None, 'wide'), parts along dimension 0
The draws below stay inside these ranges and needn't reach their ends.
There are 2 independent parts, one for each index of `groups`. The reference program is written for one: setup_inputs(seed, part) draws one part's arguments, and reference() takes and returns one part's arrays. A program takes and returns all parts, laid end to end along the dimension named above; an argument that names none is the same for every part. Nothing has to cross between parts.
All inputs are finite; a program needn't handle non-finite values.
Results may differ from the reference program's by a relative error of at most 0.015.
Values may be sent and summed in bfloat16 or wider, within the bound.
A program may use at most 192 MiB of HBM per device.

```python
import math
import jax
import jax.numpy as jnp
from jax import lax

D = 8192
HEADS = 256
HEAD_DIM = 64
STATE = 256
NGROUPS = 8
CONV = 4
SEQS = 20
INNER = 16384
BCW = 4096


def steps_of(key, shape, split, low, largest):
    def one(dim, blocks):
        steps = jax.random.uniform(jax.random.fold_in(jax.random.fold_in(key, 6), dim), (blocks,), jnp.float32, low / len(split), largest / len(split))
        return jnp.repeat(jnp.exp(steps), shape[dim] // blocks).reshape((-1,) + (1,) * (len(shape) - dim - 1))

    gain = one(*split[0])
    for cut in split[1:]:
        gain = gain * one(*cut)
    return gain


def centred(own_key, extent, spread, limit, shards=(), kind=jnp.bfloat16):
    factor_of = steps_of(own_key, extent, shards, -0.22, 0.18) if shards else 1.0
    array = jax.random.normal(own_key, extent, jnp.float32) * spread * factor_of
    return jnp.minimum(jnp.maximum(array, -limit), limit).astype(kind)


def setup_inputs(seed: int = 0, part: int = 0) -> dict:
    seeds = jax.random.split(jax.random.key(seed), 17)
    part_splits = jax.random.split(jax.random.fold_in(seeds[16], part), 17)
    inputs = centred(part_splits[0], (SEQS, 2, D), 1.0, 6.0, ((2, 4),))
    xz_weight = centred(seeds[1], (D, 2, INNER), D ** -0.5, 0.0625, ((0, 4), (2, 4)))
    bc_weight = centred(seeds[2], (D, BCW), D ** -0.5, 0.0625, ((0, 4), (1, 4)))
    dt_weight = centred(seeds[3], (D, HEADS), D ** -0.5, 0.0625, ((0, 4), (1, 4)))
    conv_x_weight = centred(seeds[4], (CONV, HEADS, HEAD_DIM), CONV ** -0.5, 3.0, ((1, 4), (2, 4)))
    conv_x_bias = centred(seeds[5], (HEADS, HEAD_DIM), 0.5, 3.0, ((0, 4), (1, 4)))
    conv_bc_weight = centred(seeds[6], (CONV, BCW), CONV ** -0.5, 3.0, ((1, 4),))
    conv_bc_bias = centred(seeds[7], (BCW,), 0.5, 3.0, ((0, 4),))
    conv_x_state = centred(part_splits[8], (SEQS, CONV - 1, HEADS, HEAD_DIM), 1.0, 6.0, ((2, 4), (3, 4)))
    conv_bc_state = centred(part_splits[9], (SEQS, CONV - 1, BCW), 1.0, 6.0, ((2, 4),))
    dt_bias = jnp.clip(-4.0 + 4.0 * jax.random.uniform(seeds[10], (HEADS,), jnp.float32) ** steps_of(seeds[10], (HEADS,), ((0, 4),), -0.2, 0.2), -4.0, 0.0)
    a_log = jnp.clip(2.5 * jax.random.uniform(seeds[11], (HEADS,), jnp.float32) ** steps_of(seeds[11], (HEADS,), ((0, 4),), -0.2, 0.2), 0.0, 2.5)
    d_skip = jnp.clip(jnp.exp(math.log(2.0) - 1.3862944 * jax.random.uniform(seeds[12], (HEADS,), jnp.float32) ** steps_of(seeds[12], (HEADS,), ((0, 4),), -0.2, 0.2)), 0.5, 2.0)
    norm_weight = jnp.clip(1.0 + 0.18 * jax.random.normal(seeds[13], (HEADS, HEAD_DIM), jnp.float32), 0.099609375, 1.8984375).astype(jnp.bfloat16)
    out_weight = centred(seeds[14], (HEADS, HEAD_DIM, D), INNER ** -0.5, 0.046875, ((1, 4), (2, 4)))
    ssm_state = centred(part_splits[15], (SEQS, HEADS, HEAD_DIM, STATE), 0.5, 4.0, ((1, 4), (2, 4)), jnp.float32)
    return dict(inputs=inputs, xz_weight=xz_weight, bc_weight=bc_weight, dt_weight=dt_weight, conv_x_weight=conv_x_weight, conv_x_bias=conv_x_bias, conv_bc_weight=conv_bc_weight, conv_bc_bias=conv_bc_bias, conv_x_state=conv_x_state, conv_bc_state=conv_bc_state, dt_bias=dt_bias, a_log=a_log, d_skip=d_skip, norm_weight=norm_weight, out_weight=out_weight, ssm_state=ssm_state)


EPSILON = 1e-05

def conv_tokens(history, fresh_vals, tap_weights, offset):
    window = jnp.concatenate([history, fresh_vals], axis=1)
    outputs = []
    for token_idx in range(2):
        summed = offset.astype(jnp.float32)
        for tap_idx in range(tap_weights.shape[0]):
            summed = summed + tap_weights[tap_idx].astype(jnp.float32) * window[:, token_idx + tap_idx].astype(jnp.float32)
        outputs.append(jax.nn.silu(summed))
    return (jnp.stack(outputs, axis=1), window[:, 2:])

def advance(ssm_now, x_tok, b_tok, c_tok, dt_tok, dt_bias, a_log, d_skip):
    step_size = jax.nn.softplus(dt_tok.astype(jnp.float32) + dt_bias)
    decay_now = jnp.exp(-step_size * jnp.exp(a_log))
    inject = (step_size[:, :, None] * x_tok)[..., None] * b_tok[:, :, None, :]
    ssm_now = decay_now[:, :, None, None] * ssm_now + inject
    readout = lax.optimization_barrier(jnp.sum(ssm_now * c_tok[:, :, None, :], axis=-1)) + d_skip[None, :, None] * x_tok
    return (ssm_now, readout)

def reference(inputs, xz_weight, bc_weight, dt_weight, conv_x_weight, conv_x_bias, conv_bc_weight, conv_bc_bias, conv_x_state, conv_bc_state, dt_bias, a_log, d_skip, norm_weight, out_weight, ssm_state):
    tok_rows = inputs.reshape(SEQS * 2, D)
    xz_proj = jnp.dot(tok_rows, xz_weight.reshape(D, 2 * INNER), preferred_element_type=jnp.float32).astype(jnp.bfloat16)
    xz_proj = xz_proj.reshape(SEQS, 2, 2, HEADS, HEAD_DIM)
    gate_vals = xz_proj[:, :, 0]
    x_proj = xz_proj[:, :, 1]
    bc_proj = jnp.dot(tok_rows, bc_weight, preferred_element_type=jnp.float32).astype(jnp.bfloat16).reshape(SEQS, 2, BCW)
    dt_proj = jnp.dot(tok_rows, dt_weight, preferred_element_type=jnp.float32).astype(jnp.bfloat16).reshape(SEQS, 2, HEADS)
    x_conv, new_conv_x = conv_tokens(conv_x_state, x_proj, conv_x_weight, conv_x_bias)
    bc_conv, new_conv_bc = conv_tokens(conv_bc_state, bc_proj, conv_bc_weight, conv_bc_bias)
    bc_groups = bc_conv.reshape(SEQS, 2, NGROUPS, 2, STATE)
    b_heads = jnp.repeat(bc_groups[:, :, :, 0], HEADS // NGROUPS, axis=2)
    c_heads = jnp.repeat(bc_groups[:, :, :, 1], HEADS // NGROUPS, axis=2)
    ssm_now = ssm_state
    readouts = []
    for token_idx in range(2):
        ssm_now, readout = advance(ssm_now, x_conv[:, token_idx], b_heads[:, token_idx], c_heads[:, token_idx], dt_proj[:, token_idx], dt_bias, a_log, d_skip)
        readouts.append(readout)
    y_all = jnp.stack(readouts, axis=1)
    gated_out = y_all * jax.nn.silu(gate_vals.astype(jnp.float32))
    grouped = gated_out.reshape(SEQS, 2, NGROUPS, HEADS // NGROUPS * HEAD_DIM)
    group_sum = lax.optimization_barrier(jnp.sum(grouped * grouped, axis=-1))
    inverse = lax.rsqrt(group_sum / (HEADS // NGROUPS * HEAD_DIM) + EPSILON)
    normed = (grouped * inverse[..., None]).reshape(SEQS, 2, HEADS, HEAD_DIM) * norm_weight.astype(jnp.float32)
    normed = normed.astype(jnp.bfloat16)
    layer_out = jnp.dot(normed.reshape(SEQS * 2, INNER), out_weight.reshape(INNER, D), preferred_element_type=jnp.float32)
    layer_out = layer_out.astype(jnp.bfloat16).reshape(SEQS, 2, D)
    return (layer_out, ssm_now, new_conv_x, new_conv_bc)
```

```python
import functools

import jax
import jax.numpy as jnp
from jax import lax
from jax.experimental import pallas as pl
from jax.experimental.pallas import tpu as pltpu
from jax.sharding import PartitionSpec as P

HEADS = 256
HEAD_DIM = 64
STATE = 256
NGROUPS = 8


EPSILON = 1e-05


def shortened(value):

    def short(part):
        return part.astype(jnp.bfloat16) if part.dtype == jnp.float32 else part

    return jax.tree.map(short, value)


def swapped(value, axis, bit):
    mask = 2**bit
    pairs = [(source, source ^ mask) for source in range(lax.axis_size(axis))]
    return lax.ppermute(value, axis, pairs)


def conv_tokens(history, fresh_vals, tap_weights, offset):
    window = jnp.concatenate([history, fresh_vals], axis=1)
    outputs = []
    for token_idx in range(2):
        summed = offset.astype(jnp.float32)
        for tap_idx in range(tap_weights.shape[0]):
            summed = summed + tap_weights[tap_idx].astype(jnp.float32) * window[
                :, token_idx + tap_idx
            ].astype(jnp.float32)
        outputs.append(jax.nn.silu(summed))
    return (jnp.stack(outputs, axis=1), window[:, 2:])


def advance(ssm_now, x_tok, b_tok, c_tok, dt_tok, dt_bias, a_log, d_skip):
    step_size = jax.nn.softplus(dt_tok.astype(jnp.float32) + dt_bias)
    decay_now = jnp.exp(-step_size * jnp.exp(a_log))
    inject = (step_size[:, :, None] * x_tok)[..., None] * b_tok[:, :, None, :]
    ssm_now = decay_now[:, :, None, None] * ssm_now + inject
    readout = jnp.sum(ssm_now * c_tok[:, :, None, :], axis=-1) + d_skip[None, :, None] * x_tok
    return (ssm_now, readout)


VMEM_BYTES = 60 << 20
MESH = pl.DeviceIdType.MESH
F32 = jnp.float32
BF16 = jnp.bfloat16


def shift_of(value):
    return value.bit_length() - 1


def greet(axes):
    barrier = pltpu.get_barrier_semaphore()
    total = 0
    for axis in axes:
        count = lax.axis_size(axis)
        me = lax.axis_index(axis)
        for hop in range(1, count):
            pl.semaphore_signal(
                barrier, inc=1, device_id={axis: lax.rem(me + hop, count)}, device_id_type=MESH
            )
        total += count - 1
    pl.semaphore_wait(barrier, total)


def project_kernel(
    slots,
    x_ref,
    dt_ref,
    w_ref,
    bc_ref,
    mine_ref,
    small_ref,
    ring,
    bc_buf,
    wide_x,
    order,
    stage,
    arrived,
    small_stage,
    small_arrived,
    ring_sem,
    bc_sem,
    send_sem,
    recv_sem,
    small_send,
    small_recv,
):
    parts = lax.axis_size("narrow")
    me = lax.axis_index("narrow")
    depth = w_ref.shape[0]
    span = 128 * parts
    blocks = w_ref.shape[2] // span
    rows = x_ref.shape[0]
    bc_columns = bc_ref.shape[1]
    dt_columns = dt_ref.shape[0]
    chan = HEAD_DIM // parts

    def fetches(block, slot):
        return [
            pltpu.make_async_copy(
                w_ref.at[:, :, pl.ds(pl.multiple_of(block * span + piece * 128, 128), 128)],
                ring.at[slot, piece],
                ring_sem.at[slot, piece],
            )
            for piece in range(parts)
        ]

    bc_copy = pltpu.make_async_copy(bc_ref, bc_buf, bc_sem)
    bc_copy.start()
    for block in range(slots):
        for copy in fetches(block, block):
            copy.start()
    source = lax.broadcasted_iota(jnp.int32, (128, 256), 0)
    target = lax.broadcasted_iota(jnp.int32, (128, 256), 1)
    spread = [(target == 2 * source + plane).astype(BF16) for plane in range(2)]
    for piece in range(depth // 128):
        part = x_ref[:, piece * 128 : (piece + 1) * 128]
        for plane in range(2):
            wide_x[plane * rows : (plane + 1) * rows, piece * 256 : (piece + 1) * 256] = jnp.dot(
                part, spread[plane], preferred_element_type=F32
            ).astype(BF16)
    column = lax.broadcasted_iota(jnp.int32, (span, span), 0)
    place = lax.broadcasted_iota(jnp.int32, (span, span), 1)
    head = lax.shift_right_logical(column, shift_of(HEAD_DIM))
    inner = lax.bitwise_and(column, HEAD_DIM - 1)
    owner = lax.shift_right_logical(inner, shift_of(chan))
    channel = lax.bitwise_and(inner, chan - 1)
    order[...] = (place == owner * 128 + head * chan + channel).astype(BF16)

    greet(("narrow",))
    small_stage[...] = jnp.zeros_like(small_stage)
    small_stage[:, bc_columns : bc_columns + dt_columns] = lax.dot_general(
        x_ref[...], dt_ref[...], (((1,), (1,)), ((), ())), preferred_element_type=F32
    ).astype(BF16)
    bc_copy.wait()
    small_stage[:, :bc_columns] = jnp.dot(
        x_ref[...], bc_buf[...], preferred_element_type=F32
    ).astype(BF16)

    def small_copy(hop):
        return pltpu.make_async_remote_copy(
            src_ref=small_stage,
            dst_ref=small_arrived.at[hop - 1],
            send_sem=small_send.at[hop - 1],
            recv_sem=small_recv.at[hop - 1],
            device_id={"narrow": lax.rem(me + hop, parts)},
            device_id_type=MESH,
        )

    def piece_copy(hop, block):
        return pltpu.make_async_remote_copy(
            src_ref=stage.at[lax.rem(me + hop, parts), block],
            dst_ref=arrived.at[hop - 1, block],
            send_sem=send_sem.at[hop - 1, block],
            recv_sem=recv_sem.at[hop - 1, block],
            device_id={"narrow": lax.rem(me + hop, parts)},
            device_id_type=MESH,
        )

    for hop in range(1, parts):
        small_copy(hop).start()

    def step(block, carry):
        slot = lax.rem(block, slots)
        for copy in fetches(block, slot):
            copy.wait()
        weights = jnp.concatenate(
            [ring[slot, piece].reshape(2 * depth, 128) for piece in range(parts)], axis=1
        )
        product = jnp.dot(wide_x[...], weights, preferred_element_type=F32).astype(BF16)

        @pl.when(block + slots < blocks)
        def _():
            for copy in fetches(block + slots, slot):
                copy.start()

        sorted_out = jnp.dot(product, order[...], preferred_element_type=F32).astype(BF16)
        for piece in range(parts):
            stage[piece, block] = sorted_out[:, piece * 128 : (piece + 1) * 128]
        for hop in range(1, parts):
            piece_copy(hop, block).start()
        return carry

    lax.fori_loop(0, blocks, step, 0)
    for hop in range(1, parts):
        small_copy(hop).wait()
    total = small_stage[...].astype(F32)
    for hop in range(1, parts):
        total = total + small_arrived[hop - 1].astype(F32)
    small_ref[...] = total.astype(BF16)
    for block in range(blocks):
        total = stage[me, block].astype(F32)
        for hop in range(1, parts):
            piece_copy(hop, block).wait()
            total = total + arrived[hop - 1, block].astype(F32)
        mine_ref[:, block * 128 : (block + 1) * 128] = total.astype(BF16)


def project(tok_rows, dt_weight, xz_weight, bc_weight):
    parts = lax.axis_size("narrow")
    rows, depth = tok_rows.shape
    blocks = xz_weight.shape[2] // (128 * parts)
    slots = min(3, blocks)
    small = bc_weight.shape[1] + 128
    vmem = pl.BlockSpec(memory_space=pltpu.VMEM)
    anywhere = pl.BlockSpec(memory_space=pl.ANY)
    return pl.pallas_call(
        functools.partial(project_kernel, slots),
        name="project",
        out_shape=(
            jax.ShapeDtypeStruct((2 * rows, 128 * blocks), BF16),
            jax.ShapeDtypeStruct((rows, small), BF16),
        ),
        in_specs=[vmem, vmem, anywhere, anywhere],
        out_specs=(vmem, vmem),
        scratch_shapes=[
            pltpu.VMEM((slots, parts, depth, 2, 128), BF16),
            pltpu.VMEM(bc_weight.shape, BF16),
            pltpu.VMEM((2 * rows, 2 * depth), BF16),
            pltpu.VMEM((128 * parts, 128 * parts), BF16),
            pltpu.VMEM((parts, blocks, 2 * rows, 128), BF16),
            pltpu.VMEM((parts - 1, blocks, 2 * rows, 128), BF16),
            pltpu.VMEM((rows, small), BF16),
            pltpu.VMEM((parts - 1, rows, small), BF16),
            pltpu.SemaphoreType.DMA((slots, parts)),
            pltpu.SemaphoreType.DMA,
            pltpu.SemaphoreType.DMA((parts - 1, blocks)),
            pltpu.SemaphoreType.DMA((parts - 1, blocks)),
            pltpu.SemaphoreType.DMA((parts - 1,)),
            pltpu.SemaphoreType.DMA((parts - 1,)),
        ],
        compiler_params=pltpu.CompilerParams(
            collective_id=0, has_side_effects=True, vmem_limit_bytes=VMEM_BYTES
        ),
    )(tok_rows, dt_weight.T, xz_weight, bc_weight)


def finish_kernel(
    groups_here,
    gated_ref,
    gain_ref,
    w_ref,
    out_ref,
    w_buf,
    squares,
    squares_in,
    normed,
    total,
    stage,
    arrived,
    w_sem,
    sq_send,
    sq_recv,
    n_send,
    n_recv,
    o_send,
    o_recv,
):
    wide = lax.axis_size("wide")
    parts = lax.axis_size("narrow")
    row = lax.axis_index("wide")
    me = lax.axis_index("narrow")
    rows, width = gated_ref.shape
    columns = w_ref.shape[1] // parts

    def fetch(hop):
        first = pl.multiple_of(lax.rem(row - hop + wide, wide) * width, width)
        return pltpu.make_async_copy(w_ref.at[pl.ds(first, width)], w_buf.at[hop], w_sem.at[hop])

    def squares_copy(hop):
        return pltpu.make_async_remote_copy(
            src_ref=squares,
            dst_ref=squares_in.at[hop - 1],
            send_sem=sq_send.at[hop - 1],
            recv_sem=sq_recv.at[hop - 1],
            device_id={"narrow": lax.rem(me + hop, parts)},
            device_id_type=MESH,
        )

    def normed_copy(hop):
        return pltpu.make_async_remote_copy(
            src_ref=normed.at[0],
            dst_ref=normed.at[hop],
            send_sem=n_send.at[hop - 1],
            recv_sem=n_recv.at[hop - 1],
            device_id={"wide": lax.rem(row + hop, wide)},
            device_id_type=MESH,
        )

    def out_copy(hop):
        return pltpu.make_async_remote_copy(
            src_ref=stage.at[lax.rem(me + hop, parts)],
            dst_ref=arrived.at[hop - 1],
            send_sem=o_send.at[hop - 1],
            recv_sem=o_recv.at[hop - 1],
            device_id={"narrow": lax.rem(me + hop, parts)},
            device_id_type=MESH,
        )

    for hop in range(wide):
        fetch(hop).start()
    greet(("narrow", "wide"))
    gated = gated_ref[...]
    if groups_here:
        share = width // groups_here
        lane = lax.broadcasted_iota(jnp.int32, (rows, 128), 1)
        sums = jnp.zeros((rows, 128), F32)
        for group in range(groups_here):
            cut = gated[:, group * share : (group + 1) * share]
            sums = jnp.where(lane == group, jnp.sum(cut * cut, axis=1, keepdims=True), sums)
        squares[...] = sums
        for hop in range(1, parts):
            squares_copy(hop).start()
        for hop in range(1, parts):
            squares_copy(hop).wait()
            sums = sums + squares_in[hop - 1]
        inverse = lax.rsqrt(sums / (HEADS // NGROUPS * HEAD_DIM) + EPSILON)
        for group in range(groups_here):
            cut = slice(group * share, (group + 1) * share)
            normed[0, :, cut] = (
                gated[:, cut] * inverse[:, group : group + 1] * gain_ref[:, cut]
            ).astype(BF16)
    else:
        normed[0] = (gated * gain_ref[...]).astype(BF16)
    for hop in range(1, wide):
        normed_copy(hop).start()
    for hop in range(wide):
        fetch(hop).wait()
        if hop:
            normed_copy(hop).wait()
        part = jnp.dot(normed[hop], w_buf[hop], preferred_element_type=F32)
        if hop:
            part = part + total[...]
        if hop < wide - 1:
            total[...] = part
        else:
            for piece in range(parts):
                stage[piece] = part[:, piece * columns : (piece + 1) * columns].astype(BF16)
    for hop in range(1, parts):
        out_copy(hop).start()
    final = stage[me].astype(F32)
    for hop in range(1, parts):
        out_copy(hop).wait()
        final = final + arrived[hop - 1].astype(F32)
    out_ref[...] = final.astype(BF16)


def finish(gated, gain, out_weight, groups_here):
    parts = lax.axis_size("narrow")
    wide = lax.axis_size("wide")
    rows, width = gated.shape
    columns = out_weight.shape[1] // parts
    vmem = pl.BlockSpec(memory_space=pltpu.VMEM)
    return pl.pallas_call(
        functools.partial(finish_kernel, groups_here),
        name="finish",
        out_shape=jax.ShapeDtypeStruct((rows, columns), BF16),
        in_specs=[vmem, vmem, pl.BlockSpec(memory_space=pl.ANY)],
        out_specs=vmem,
        scratch_shapes=[
            pltpu.VMEM((wide, width, out_weight.shape[1]), BF16),
            pltpu.VMEM((rows, 128), F32),
            pltpu.VMEM((parts - 1, rows, 128), F32),
            pltpu.VMEM((wide, rows, width), BF16),
            pltpu.VMEM((rows, out_weight.shape[1]), F32),
            pltpu.VMEM((parts, rows, columns), BF16),
            pltpu.VMEM((parts - 1, rows, columns), BF16),
            pltpu.SemaphoreType.DMA((wide,)),
            pltpu.SemaphoreType.DMA((parts - 1,)),
            pltpu.SemaphoreType.DMA((parts - 1,)),
            pltpu.SemaphoreType.DMA((wide - 1,)),
            pltpu.SemaphoreType.DMA((wide - 1,)),
            pltpu.SemaphoreType.DMA((parts - 1,)),
            pltpu.SemaphoreType.DMA((parts - 1,)),
        ],
        compiler_params=pltpu.CompilerParams(
            collective_id=1, has_side_effects=True, vmem_limit_bytes=VMEM_BYTES
        ),
    )(gated, gain, out_weight)


def shards(
    inputs,
    xz_weight,
    bc_weight,
    dt_weight,
    conv_x_weight,
    conv_x_bias,
    conv_bc_weight,
    conv_bc_bias,
    conv_x_state,
    conv_bc_state,
    dt_bias,
    a_log,
    d_skip,
    norm_weight,
    out_weight,
    ssm_state,
):
    seq_count = inputs.shape[0]
    row_count = seq_count * 2
    tok_rows = inputs.reshape(row_count, inputs.shape[2])
    head_local = dt_weight.shape[1]
    wide_count = lax.axis_size("wide")
    narrow_count = lax.axis_size("narrow")
    wide_index = lax.axis_index("wide")
    chan_local = HEAD_DIM // narrow_count
    xz_mine, small = project(tok_rows, dt_weight, xz_weight, bc_weight)
    bc_summed = small[:, : bc_weight.shape[1]]
    dt_summed = small[:, bc_weight.shape[1] : bc_weight.shape[1] + head_local]
    xz_mine = xz_mine.reshape(2, seq_count, 2, head_local, chan_local)
    gate_vals = xz_mine[0]
    x_proj = xz_mine[1]
    bc_proj = bc_summed.reshape(seq_count, 2, bc_summed.shape[1])
    dt_proj = dt_summed.reshape(seq_count, 2, head_local)
    x_conv, new_conv_x = conv_tokens(conv_x_state, x_proj, conv_x_weight, conv_x_bias)
    bc_conv, new_conv_bc = conv_tokens(conv_bc_state, bc_proj, conv_bc_weight, conv_bc_bias)
    group_local = max(NGROUPS // wide_count, 1)
    group_span = max(wide_count // NGROUPS, 1)
    bc_mine = bc_conv.reshape(row_count, bc_conv.shape[2])
    for bit_idx in range(group_span.bit_length() - 1):
        partner = swapped(shortened(bc_mine), "wide", bit_idx).astype(bc_mine.dtype)
        is_lower = wide_index // (1 << bit_idx) % 2 == 0
        bc_mine = jnp.where(
            is_lower,
            jnp.concatenate([bc_mine, partner], axis=1),
            jnp.concatenate([partner, bc_mine], axis=1),
        )
    bc_heads = bc_mine.reshape(seq_count, 2, group_local, 2, STATE)
    per_group = head_local // group_local
    b_heads = jnp.repeat(bc_heads[:, :, :, 0], per_group, axis=2)
    c_heads = jnp.repeat(bc_heads[:, :, :, 1], per_group, axis=2)
    ssm_now = ssm_state
    readouts = []
    for token_idx in range(2):
        ssm_now, readout = advance(
            ssm_now,
            x_conv[:, token_idx],
            b_heads[:, token_idx],
            c_heads[:, token_idx],
            dt_proj[:, token_idx],
            dt_bias,
            a_log,
            d_skip,
        )
        readouts.append(readout)
    y_all = jnp.stack(readouts, axis=1)
    gated_out = y_all * jax.nn.silu(gate_vals.astype(jnp.float32))
    gain = norm_weight.astype(jnp.float32).reshape(1, head_local * chan_local)
    gated_rows = gated_out.reshape(row_count, head_local * chan_local)
    if group_span > 1:
        group_sum = lax.psum(jnp.sum(gated_rows * gated_rows, axis=1, keepdims=True), "narrow")
        for bit_idx in range(group_span.bit_length() - 1):
            group_sum = group_sum + swapped(group_sum, "wide", bit_idx)
        gated_rows = gated_rows * lax.rsqrt(group_sum / (HEADS // NGROUPS * HEAD_DIM) + EPSILON)
    out_mine = finish(
        gated_rows,
        gain,
        out_weight.reshape(-1, out_weight.shape[2]),
        group_local if group_span == 1 else 0,
    )
    layer_out = out_mine.reshape(seq_count, 2, out_mine.shape[1])
    return (layer_out, ssm_now, new_conv_x, new_conv_bc)


def solution(mesh):
    return jax.shard_map(
        shards,
        mesh=mesh,
        in_specs=(
            P("groups", None, "narrow"),
            P("narrow", None, "wide"),
            P("narrow", "wide"),
            P("narrow", "wide"),
            P(None, "wide", "narrow"),
            P("wide", "narrow"),
            P(None, "wide"),
            P("wide"),
            P("groups", None, "wide", "narrow"),
            P("groups", None, "wide"),
            P("wide"),
            P("wide"),
            P("wide"),
            P("wide", "narrow"),
            P(None, "narrow", "wide"),
            P("groups", "wide", "narrow", None),
        ),
        out_specs=(
            P("groups", None, ("wide", "narrow")),
            P("groups", "wide", "narrow", None),
            P("groups", None, "wide", "narrow"),
            P("groups", None, "wide"),
        ),
        check_vma=False,
    )
```
